32 devices in a mesh: user: 4 (over x, core), heads: 2 (over y), ctx: 4 (over z).
Axes of the slice: x: 2, y: 2, z: 4, core: 2. Of those that a mesh axis runs over, the one named last changes fastest.
Arguments:
- keys: bfloat16 [65536, 512], P(('user', 'ctx'), 'heads'), parts along dimension 0, may hold values from -6 to 6
- values: bfloat16 [65536, 512], P(('user', 'ctx'), 'heads'), parts along dimension 0, may hold values from -6 to 6
- queries: bfloat16 [4, 12288, 128], P('heads', ('user', 'ctx')), parts along dimension 1, may hold values from -240 to 240
- positions: int32 [12288], P(('user', 'ctx')), parts along dimension 0, may hold values from 0 to 16383
Outputs:
- attended: bfloat16 [4, 12288, 128], P('heads', ('user', 'ctx')), parts along dimension 1
The draws below stay inside these ranges and needn't reach their ends.
There are 4 independent parts, one for each index of `user`. The reference program is written for one: setup_inputs(seed, part) draws one part's arguments, and reference() takes and returns one part's arrays. A program takes and returns all parts, laid end to end along the dimension named above; each array names one. Nothing has to cross between parts.
All inputs are finite; a program needn't handle non-finite values.
Results may differ from the reference program's by a relative error of at most 0.008.
The reference program's roundings to bfloat16 on the way count: a program that leaves them out, or rounds other values in their place, can miss the bound.
Values may be sent and summed in bfloat16 or wider, within the bound.
A program may use at most 128 MiB of HBM per device.

```python
import math
import jax
import jax.numpy as jnp
from jax import lax

WINDOW = 16384
KV_HEADS = 4
HEAD_DIM = 128
QUERY_DEV = 768
QUERIES = 3072


def draw_queries(key, part):
    first_key = jax.random.fold_in(jax.random.fold_in(key, 11), 0)
    base = jax.random.truncated_normal(first_key, -4.0, 4.0, (KV_HEADS, QUERIES, HEAD_DIM), jnp.float32)
    return base.astype(jnp.bfloat16)


def set_ends(drawn, key, low, largest):
    spot = [jax.random.randint(jax.random.fold_in(key, axis), (), 0, length) for axis, length in enumerate(drawn.shape)]
    main_axis = drawn.shape.index(max(drawn.shape))
    next_to = spot[:main_axis] + [(spot[main_axis] + 1) % drawn.shape[main_axis]] + spot[main_axis + 1:]
    return drawn.at[tuple(spot)].set(low).at[tuple(next_to)].set(largest)


def steps_of(own_key, extent, shards, smallest, high):
    loudness = 1.0
    for axis_at, parts in shards:
        heights = jax.random.uniform(jax.random.fold_in(jax.random.fold_in(own_key, 6), axis_at), (parts,), jnp.float32, smallest / len(shards), high / len(shards))
        loudness = loudness * jnp.repeat(jnp.exp(heights), extent[axis_at] // parts).reshape((-1,) + (1,) * (len(extent) - 1 - axis_at))
    return loudness


def normal_values(stream_key, extent, deviation, most, cuts=(), kind=jnp.bfloat16):
    entries = deviation * jax.random.normal(stream_key, extent, jnp.float32)
    if cuts:
        entries = entries * steps_of(stream_key, extent, cuts, -0.22, 0.18)
    return jnp.clip(entries, -most, most).astype(kind)


def setup_inputs(seed: int = 0, part: int = 0) -> dict:
    seeds = jax.random.split(jax.random.key(seed), 5)
    part_keys = jax.random.split(jax.random.fold_in(seeds[4], part), 5)
    keys = normal_values(part_keys[0], (WINDOW, KV_HEADS * HEAD_DIM), 1.0, 6.0, ((0, 4), (1, 2)))
    values = normal_values(part_keys[1], (WINDOW, KV_HEADS * HEAD_DIM), 1.0, 6.0, ((0, 4), (1, 2)))
    queries = draw_queries(jax.random.fold_in(jax.random.fold_in(seeds[4], part), 71), part)
    positions = set_ends(jax.random.randint(part_keys[3], (QUERIES,), 0, WINDOW), jax.random.fold_in(part_keys[3], 1), 0, WINDOW - 1).astype(jnp.int32)
    return {"keys": keys, "values": values, "queries": queries, "positions": positions}


def compress(signal):
    length = signal.shape[0]
    reordered = jnp.concatenate([signal[0::2], signal[1::2][::-1]], axis=0)
    spectrum = jnp.fft.fft(reordered, axis=0)
    index = jnp.arange(length // 2).astype(jnp.float32)[:, None]
    kept = spectrum[:length // 2]
    coeffs = jnp.real(kept) * jnp.cos(math.pi * index / (2 * length)) + jnp.imag(kept) * jnp.sin(math.pi * index / (2 * length))
    weight = jnp.where(index == 0.0, 1.0 / length, 2.0 / length)
    scaled = coeffs * weight
    twisted = lax.complex(scaled * jnp.cos(math.pi * index / length), scaled * jnp.sin(math.pi * index / length))
    padded = jnp.concatenate([twisted, jnp.zeros_like(twisted)], axis=0)
    return jnp.real(jnp.fft.ifft(padded, axis=0))[:length // 2] * length

def inverse_freq(width):
    return jnp.exp(jnp.arange(width // 2).astype(jnp.float32) * (-2.0 * math.log(500000.0) / width))

def rotate_rows(block, places):
    width = block.shape[-1]
    half = width // 2
    angles = places[:, None] * inverse_freq(width)[None, :]
    cosine = jnp.cos(angles)
    sine = jnp.sin(angles)
    first = block[..., :half]
    second = block[..., half:]
    return jnp.concatenate([first * cosine - second * sine, second * cosine + first * sine], axis=-1)

def reference(keys, values, queries, positions):
    key_small = compress(keys.astype(jnp.float32)).astype(jnp.bfloat16)
    value_small = compress(values.astype(jnp.float32)).astype(jnp.bfloat16)
    kept_len = key_small.shape[0]
    places = jnp.arange(kept_len).astype(jnp.float32)
    query_places = positions.astype(jnp.float32)
    scaling = 1.0 / math.sqrt(HEAD_DIM)
    results = []
    for head_index in range(KV_HEADS):
        low = head_index * HEAD_DIM
        key_head = rotate_rows(key_small[:, low:low + HEAD_DIM].astype(jnp.float32), places).astype(jnp.bfloat16)
        value_head = value_small[:, low:low + HEAD_DIM]
        query_head = rotate_rows(queries[head_index].astype(jnp.float32), query_places).astype(jnp.bfloat16)
        blocks = query_head.reshape(QUERIES // QUERY_DEV, QUERY_DEV, HEAD_DIM)

        def attend_block(query_block):
            scores = jnp.dot(query_block, key_head.T, preferred_element_type=jnp.float32) * scaling
            top = lax.optimization_barrier(jnp.max(scores, axis=1, keepdims=True))
            expo = jnp.exp(scores - top)
            denom = lax.optimization_barrier(jnp.sum(expo, axis=1, keepdims=True))
            summed = jnp.dot(expo.astype(jnp.bfloat16), value_head, preferred_element_type=jnp.float32)
            return (summed / denom).astype(jnp.bfloat16)
        results.append(lax.map(attend_block, blocks).reshape(QUERIES, HEAD_DIM))
    return jnp.stack(results)
```

```python
import functools
import math

import jax
import jax.numpy as jnp
import numpy as np
from jax import lax
from jax.experimental import pallas as pl
from jax.experimental.pallas import tpu as pltpu
from jax.sharding import PartitionSpec as P

OUTER = 128


def split_two(matrix):
    high = matrix.astype(jnp.bfloat16)
    low = (matrix - np.asarray(high).astype(np.float64)).astype(jnp.bfloat16)
    return high, low


@functools.lru_cache(maxsize=None)
def stages(length):
    outer = OUTER
    inner = length // outer
    step = inner // 2
    a = np.arange(outer)
    c = np.arange(outer)
    turn = 2 * outer
    angle = np.pi / outer * ((c[:, None] * a[None, :]) % turn)
    alternate = np.where(a % 2 == 0, 1.0, -1.0)
    first = np.stack([np.cos(angle), -np.sin(angle)], axis=1)
    first[0, 1] = alternate
    d = np.arange(length // 2 // turn)
    k = np.concatenate([c[:, None] + turn * d, (turn - c[:, None]) % turn + turn * d], axis=1)
    k[0, d.size :] = outer + turn * d
    sign = np.concatenate([np.ones(d.size), -np.ones(d.size)])
    b = np.arange(inner)
    q = np.arange(step)
    theta = np.pi / (2 * length) * ((k[:, :, None] * (2 * b + 1)) % (4 * length))
    phi = np.pi / length * ((k[:, None, :] * (2 * q + 1)[:, None]) % (2 * length))
    forward = np.stack([np.cos(theta), np.sin(theta) * sign[None, :, None]], axis=2)
    weight = np.where(k == 0, 1.0, 2.0) / length
    back = np.stack([np.cos(phi), np.sin(phi) * sign], axis=1) * weight[:, None, None, :]
    half = d.size
    forward[0, :half, 1] = 0.0
    forward[0, half:, 1] = np.cos(theta[0, half:])
    forward[0, half:, 0] = 0.0
    back[0, 1, :, :half] = 0.0
    back[0, 1, :, half:] = np.cos(phi[0, :, half:]) * weight[0, half:]
    back[0, 0, :, half:] = 0.0
    middle = back.reshape(outer, 2 * step, 2 * half) @ forward.reshape(outer, 2 * half, 2 * inner)
    last = first.transpose(2, 0, 1).reshape(outer, 2 * outer)
    return first.reshape(2 * outer, outer), middle, last


def compress(signal):
    length, columns = signal.shape
    outer, inner = OUTER, length // OUTER
    first, middle, last = stages(length)
    first_high, first_low = split_two(first)
    flat = signal.reshape(outer, inner * columns)
    one = jnp.dot(first_high, flat, preferred_element_type=jnp.float32) + jnp.dot(
        first_low, flat, preferred_element_type=jnp.float32
    )
    one = one.reshape(outer, 2 * inner, columns)
    two = jnp.einsum(
        "cob,cbl->col", jnp.asarray(middle.astype(np.float32)), one, precision=lax.Precision.HIGH
    )
    three = jnp.dot(
        jnp.asarray(last.astype(np.float32)),
        two.reshape(2 * outer, inner // 2 * columns),
        precision=lax.Precision.HIGH,
    )
    return three.reshape(length // 2, columns).astype(jnp.bfloat16)


def inverse_freq(width):
    return jnp.exp(jnp.arange(width // 2).astype(jnp.float32) * (-2.0 * math.log(500000.0) / width))


def rotate_rows(block, places):
    width = block.shape[-1]
    half = width // 2
    angles = places[:, None] * inverse_freq(width)[None, :]
    cosine = jnp.cos(angles)
    sine = jnp.sin(angles)
    first = block[..., :half]
    second = block[..., half:]
    return jnp.concatenate(
        [first * cosine - second * sine, second * cosine + first * sine], axis=-1
    )


def attend_kernel(chunk, scale, q_ref, k_ref, v_ref, out_ref, lse_ref):
    q = q_ref[0]
    rows, width = q.shape
    factor = scale * math.log2(math.e)
    best = jnp.full((rows, 1), -jnp.inf, jnp.float32)
    total = jnp.zeros((rows, 1), jnp.float32)
    accum = jnp.zeros((rows, width), jnp.float32)
    tokens = k_ref.shape[1]
    for start in range(0, tokens, chunk):
        k = k_ref[0, start : start + chunk, :]
        v = v_ref[0, start : start + chunk, :]
        scores = lax.dot_general(
            q, k, (((1,), (1,)), ((), ())), preferred_element_type=jnp.float32
        )
        fresh = jnp.maximum(best, jnp.max(scores, axis=1, keepdims=True))
        expo = jnp.exp2((scores - fresh) * factor)
        shrink = jnp.exp2((best - fresh) * factor)
        total = total * shrink + jnp.sum(expo, axis=1, keepdims=True)
        accum = accum * shrink + jnp.dot(
            expo.astype(jnp.bfloat16), v, preferred_element_type=jnp.float32
        )
        best = fresh
    out_ref[0] = (accum / total).astype(out_ref.dtype)
    lse_ref[0] = jnp.broadcast_to(best * factor + jnp.log2(total), (rows, 8))


def attend(queries, keys, values):
    groups, rows, width = queries.shape
    heads, tokens, _ = keys.shape
    per_head = groups // heads
    block = math.gcd(rows, 256)
    chunk = math.gcd(tokens, 1024)
    scale = 1.0 / math.sqrt(width)
    return pl.pallas_call(
        functools.partial(attend_kernel, chunk, scale),
        grid=(groups, rows // block),
        in_specs=[
            pl.BlockSpec((1, block, width), lambda g, i: (g, i, 0)),
            pl.BlockSpec((1, tokens, width), lambda g, i: (g // per_head, 0, 0)),
            pl.BlockSpec((1, tokens, width), lambda g, i: (g // per_head, 0, 0)),
        ],
        out_specs=[
            pl.BlockSpec((1, block, width), lambda g, i: (g, i, 0)),
            pl.BlockSpec((1, block, 8), lambda g, i: (g, i, 0)),
        ],
        out_shape=[
            jax.ShapeDtypeStruct((groups, rows, width), jnp.bfloat16),
            jax.ShapeDtypeStruct((groups, rows, 8), jnp.float32),
        ],
        cost_estimate=pl.CostEstimate(
            flops=4 * groups * rows * tokens * width,
            bytes_accessed=2 * groups * rows * width * 2,
            transcendentals=groups * rows * tokens,
        ),
    )(queries, keys, values)


def by_pairs(keys, values, queries, positions, count):
    heads, rows, width = queries.shape
    me = lax.axis_index("ctx")
    odd = me % 2 == 1
    pieces = []
    for head in range(heads):
        pieces.append(keys[:, head * width : (head + 1) * width])
        pieces.append(values[:, head * width : (head + 1) * width])
    mine = lax.all_to_all(jnp.stack(pieces), "ctx", split_axis=0, concat_axis=0, tiled=True)
    rotated = rotate_rows(queries.astype(jnp.float32), positions.astype(jnp.float32)).astype(
        jnp.bfloat16
    )
    asked = lax.all_to_all(
        jnp.repeat(rotated, 2, axis=0), "ctx", split_axis=0, concat_axis=0, tiled=True
    )
    compact = compress(mine.reshape(-1, width))
    tokens = compact.shape[0]
    half = tokens // 2
    low, high = compact[:half], compact[half:]
    places = (jnp.arange(half) + jnp.where(odd, half, 0)).astype(jnp.float32)
    other = lax.ppermute(
        jnp.where(odd, low, high), "ctx", [(i, i ^ 1) for i in range(count)]
    )
    key_rows = jnp.where(odd, other, low)
    value_rows = jnp.where(odd, high, other)
    ready = rotate_rows(key_rows.astype(jnp.float32), places).astype(jnp.bfloat16)
    part, lse = attend(asked, ready[None], value_rows[None])
    lse = lse[:, :, 0].reshape(count, rows // width, width)
    top = lax.reduce_precision(lse, 8, 7)
    rest = lse - top
    mid = lax.reduce_precision(rest, 8, 7)
    last = (rest - mid).astype(jnp.bfloat16)
    top, mid = top.astype(jnp.bfloat16), mid.astype(jnp.bfloat16)
    sent = lax.all_to_all(
        jnp.concatenate([part, top, mid, last], axis=1),
        "ctx",
        split_axis=0,
        concat_axis=0,
        tiled=True,
    )
    got = sent[:, :rows].astype(jnp.float32).reshape(heads, 2, rows, width)
    logs = jnp.sum(
        sent[:, rows:].astype(jnp.float32).reshape(heads, 2, 3, rows), axis=2
    )
    share = jax.nn.sigmoid((logs[:, 0] - logs[:, 1]) * math.log(2.0))[..., None]
    return (got[:, 0] * share + got[:, 1] * (1.0 - share)).astype(jnp.bfloat16)


def by_columns(keys, values, queries, positions):
    key_parts = lax.all_to_all(keys, "ctx", split_axis=1, concat_axis=0, tiled=True)
    value_parts = lax.all_to_all(values, "ctx", split_axis=1, concat_axis=0, tiled=True)
    heads, rows, width = queries.shape
    per_device = key_parts.shape[1]
    compact = compress(jnp.concatenate([key_parts, value_parts], axis=1))
    rotated = rotate_rows(queries.astype(jnp.float32), positions.astype(jnp.float32)).astype(
        jnp.bfloat16
    )
    whole = lax.all_gather(compact.T, "ctx", axis=0, tiled=True)
    tokens = whole.shape[1]
    shaped = whole.reshape(-1, 2, per_device, tokens)
    key_rows = shaped[:, 0].reshape(heads, width, tokens).swapaxes(1, 2)
    value_rows = shaped[:, 1].reshape(heads, width, tokens).swapaxes(1, 2)
    places = jnp.arange(tokens).astype(jnp.float32)
    ready = rotate_rows(key_rows.astype(jnp.float32), places).astype(jnp.bfloat16)
    return attend(rotated, ready, value_rows)[0]


def solution(mesh):
    count = mesh.shape["ctx"]

    def on_device(keys, values, queries, positions):
        heads, rows, width = queries.shape
        if count == 2 * heads and rows % width == 0:
            return by_pairs(keys, values, queries, positions, count)
        return by_columns(keys, values, queries, positions)

    return jax.shard_map(
        on_device,
        mesh=mesh,
        in_specs=(
            P(("user", "ctx"), "heads"),
            P(("user", "ctx"), "heads"),
            P("heads", ("user", "ctx"), None),
            P(("user", "ctx")),
        ),
        out_specs=P("heads", ("user", "ctx"), None),
        check_vma=False,
    )
```

```python
import functools
import math

import jax
import jax.numpy as jnp
import numpy as np
from jax import lax
from jax.experimental import pallas as pl
from jax.experimental.pallas import tpu as pltpu
from jax.sharding import PartitionSpec as P

OUTER = 128


def split_two(matrix):
    high = matrix.astype(jnp.bfloat16)
    low = (matrix - np.asarray(high).astype(np.float64)).astype(jnp.bfloat16)
    return high, low


@functools.lru_cache(maxsize=None)
def stages(length):
    outer = OUTER
    inner = length // outer
    step = inner // 2
    a = np.arange(outer)
    c = np.arange(outer)
    turn = 2 * outer
    angle = np.pi / outer * ((c[:, None] * a[None, :]) % turn)
    alternate = np.where(a % 2 == 0, 1.0, -1.0)
    first = np.stack([np.cos(angle), -np.sin(angle)], axis=1)
    first[0, 1] = alternate
    d = np.arange(length // 2 // turn)
    k = np.concatenate([c[:, None] + turn * d, (turn - c[:, None]) % turn + turn * d], axis=1)
    k[0, d.size :] = outer + turn * d
    sign = np.concatenate([np.ones(d.size), -np.ones(d.size)])
    b = np.arange(inner)
    q = np.arange(step)
    theta = np.pi / (2 * length) * ((k[:, :, None] * (2 * b + 1)) % (4 * length))
    phi = np.pi / length * ((k[:, None, :] * (2 * q + 1)[:, None]) % (2 * length))
    forward = np.stack([np.cos(theta), np.sin(theta) * sign[None, :, None]], axis=2)
    weight = np.where(k == 0, 1.0, 2.0) / length
    back = np.stack([np.cos(phi), np.sin(phi) * sign], axis=1) * weight[:, None, None, :]
    half = d.size
    forward[0, :half, 1] = 0.0
    forward[0, half:, 1] = np.cos(theta[0, half:])
    forward[0, half:, 0] = 0.0
    back[0, 1, :, :half] = 0.0
    back[0, 1, :, half:] = np.cos(phi[0, :, half:]) * weight[0, half:]
    back[0, 0, :, half:] = 0.0
    middle = back.reshape(outer, 2 * step, 2 * half) @ forward.reshape(outer, 2 * half, 2 * inner)
    last = first.transpose(2, 0, 1).reshape(outer, 2 * outer)
    return first.reshape(2 * outer, outer), middle, last


def compress(signal):
    length, columns = signal.shape
    outer, inner = OUTER, length // OUTER
    first, middle, last = stages(length)
    first_high, first_low = split_two(first)
    flat = signal.reshape(outer, inner * columns)
    one = jnp.dot(first_high, flat, preferred_element_type=jnp.float32) + jnp.dot(
        first_low, flat, preferred_element_type=jnp.float32
    )
    one = one.reshape(outer, 2 * inner, columns)
    two = jnp.einsum(
        "cob,cbl->col", jnp.asarray(middle.astype(np.float32)), one, precision=lax.Precision.HIGH
    )
    three = jnp.dot(
        jnp.asarray(last.astype(np.float32)),
        two.reshape(2 * outer, inner // 2 * columns),
        precision=lax.Precision.HIGH,
    )
    return three.reshape(length // 2, columns).astype(jnp.bfloat16)

GAP = 8


def strict_dot(left_high, left_low, right):
    high = right.astype(jnp.bfloat16)
    low = (right - high.astype(jnp.float32)).astype(jnp.bfloat16)
    dot = functools.partial(jnp.dot, preferred_element_type=jnp.float32)
    return dot(left_high, high) + (dot(left_high, low) + dot(left_low, high))


def compress_kernel(
    inner, x_ref, first_ref, high_ref, low_ref, last_high_ref, last_low_ref, y_ref, wide_ref, one_ref
):
    outer = OUTER
    step = inner // 2
    here = pl.program_id(0)
    steps = pl.num_programs(0)
    per_step = high_ref.shape[0]
    x_pitch = inner + GAP
    one_pitch = 2 * outer + GAP
    two_pitch = step + GAP

    @pl.when(here == 0)
    def _():
        def widen(a, carry):
            source = pl.multiple_of(a * inner, inner)
            wide_ref[pl.ds(pl.multiple_of(a * x_pitch, GAP), inner), :] = x_ref[
                pl.ds(source, inner), :
            ].astype(jnp.float32)
            return carry

        lax.fori_loop(0, outer, widen, 0, unroll=2)

        def stage_one(b, carry):
            x = wide_ref[pl.ds(b, outer, stride=x_pitch), :].astype(jnp.bfloat16)
            both = jnp.concatenate([x, x], axis=0)
            one_ref[pl.ds(pl.multiple_of(b * one_pitch, GAP), 2 * outer), :] = jnp.dot(
                first_ref[...], both, preferred_element_type=jnp.float32
            )
            return carry

        lax.fori_loop(0, inner, stage_one, 0, unroll=4)

    for i in range(per_step):
        c = here * per_step + i
        z = jnp.concatenate(
            [
                one_ref[pl.ds(2 * c, inner, stride=one_pitch), :],
                one_ref[pl.ds(2 * c + 1, inner, stride=one_pitch), :],
            ],
            axis=0,
        )
        v = strict_dot(high_ref[i], low_ref[i], z)
        for part in range(2):
            wide_ref[pl.ds(pl.multiple_of((2 * c + part) * two_pitch, GAP), step), :] = v[
                part * step : (part + 1) * step
            ]

    @pl.when(here == steps - 1)
    def _():
        def stage_three(q, carry):
            v = wide_ref[pl.ds(q, 2 * outer, stride=two_pitch), :]
            y = strict_dot(last_high_ref[...], last_low_ref[...], v)
            y_ref[pl.ds(pl.multiple_of(q * outer, outer), outer), :] = y.astype(y_ref.dtype)
            return carry

        lax.fori_loop(0, step, stage_three, 0, unroll=4)


def compress_rows(signal):
    length, columns = signal.shape
    outer, inner = OUTER, length // OUTER
    first, middle, last = stages(length)
    first_pair = np.concatenate(split_two(first), axis=1)
    middle_high, middle_low = split_two(middle)
    last_high, last_low = split_two(last)
    per_step = 8
    rows_wide = max(outer * (inner + GAP), 2 * outer * (inner // 2 + GAP))
    once = pl.BlockSpec(memory_space=pltpu.VMEM)
    block = pl.BlockSpec((per_step, inner, 2 * inner), lambda i: (i, 0, 0))
    return pl.pallas_call(
        functools.partial(compress_kernel, inner),
        grid=(outer // per_step,),
        in_specs=[once, once, block, block, once, once],
        out_specs=once,
        out_shape=jax.ShapeDtypeStruct((length // 2, columns), jnp.bfloat16),
        scratch_shapes=[
            pltpu.VMEM((rows_wide, columns), jnp.float32),
            pltpu.VMEM((inner * (2 * outer + GAP), columns), jnp.float32),
        ],
        cost_estimate=pl.CostEstimate(
            flops=16 * length * outer * columns, bytes_accessed=6 * length * columns, transcendentals=0
        ),
    )(signal, first_pair, middle_high, middle_low, last_high, last_low)


def inverse_freq(width):
    return jnp.exp(jnp.arange(width // 2).astype(jnp.float32) * (-2.0 * math.log(500000.0) / width))


def rotate_rows(block, places):
    width = block.shape[-1]
    half = width // 2
    angles = places[:, None] * inverse_freq(width)[None, :]
    cosine = jnp.cos(angles)
    sine = jnp.sin(angles)
    first = block[..., :half]
    second = block[..., half:]
    return jnp.concatenate(
        [first * cosine - second * sine, second * cosine + first * sine], axis=-1
    )


def attend_kernel(chunk, scale, q_ref, k_ref, v_ref, out_ref, lse_ref):
    q = q_ref[0]
    rows, width = q.shape
    factor = scale * math.log2(math.e)
    best = jnp.full((rows, 1), -jnp.inf, jnp.float32)
    total = jnp.zeros((rows, 1), jnp.float32)
    accum = jnp.zeros((rows, width), jnp.float32)
    tokens = k_ref.shape[1]
    for start in range(0, tokens, chunk):
        k = k_ref[0, start : start + chunk, :]
        v = v_ref[0, start : start + chunk, :]
        scores = lax.dot_general(
            q, k, (((1,), (1,)), ((), ())), preferred_element_type=jnp.float32
        )
        fresh = jnp.maximum(best, jnp.max(scores, axis=1, keepdims=True))
        expo = jnp.exp2((scores - fresh) * factor)
        shrink = jnp.exp2((best - fresh) * factor)
        total = total * shrink + jnp.sum(expo, axis=1, keepdims=True)
        accum = accum * shrink + jnp.dot(
            expo.astype(jnp.bfloat16), v, preferred_element_type=jnp.float32
        )
        best = fresh
    out_ref[0] = (accum / total).astype(out_ref.dtype)
    lse_ref[0] = jnp.broadcast_to(best * factor + jnp.log2(total), (rows, 8))


def attend(queries, keys, values):
    groups, rows, width = queries.shape
    heads, tokens, _ = keys.shape
    per_head = groups // heads
    block = math.gcd(rows, 256)
    chunk = math.gcd(tokens, 1024)
    scale = 1.0 / math.sqrt(width)
    return pl.pallas_call(
        functools.partial(attend_kernel, chunk, scale),
        grid=(groups, rows // block),
        in_specs=[
            pl.BlockSpec((1, block, width), lambda g, i: (g, i, 0)),
            pl.BlockSpec((1, tokens, width), lambda g, i: (g // per_head, 0, 0)),
            pl.BlockSpec((1, tokens, width), lambda g, i: (g // per_head, 0, 0)),
        ],
        out_specs=[
            pl.BlockSpec((1, block, width), lambda g, i: (g, i, 0)),
            pl.BlockSpec((1, block, 8), lambda g, i: (g, i, 0)),
        ],
        out_shape=[
            jax.ShapeDtypeStruct((groups, rows, width), jnp.bfloat16),
            jax.ShapeDtypeStruct((groups, rows, 8), jnp.float32),
        ],
        cost_estimate=pl.CostEstimate(
            flops=4 * groups * rows * tokens * width,
            bytes_accessed=2 * groups * rows * width * 2,
            transcendentals=groups * rows * tokens,
        ),
    )(queries, keys, values)


def by_pairs(keys, values, queries, positions, count):
    heads, rows, width = queries.shape
    me = lax.axis_index("ctx")
    odd = me % 2 == 1
    pieces = []
    for head in range(heads):
        pieces.append(keys[:, head * width : (head + 1) * width])
        pieces.append(values[:, head * width : (head + 1) * width])
    mine = lax.all_to_all(jnp.stack(pieces), "ctx", split_axis=0, concat_axis=0, tiled=True)
    rotated = rotate_rows(queries.astype(jnp.float32), positions.astype(jnp.float32)).astype(
        jnp.bfloat16
    )
    asked = lax.all_to_all(
        jnp.repeat(rotated, 2, axis=0), "ctx", split_axis=0, concat_axis=0, tiled=True
    )
    compact = compress_rows(mine.reshape(-1, width))
    tokens = compact.shape[0]
    half = tokens // 2
    low, high = compact[:half], compact[half:]
    at = jnp.arange(half) + jnp.where(odd, half, 0)
    places = (at % OUTER * (tokens // OUTER) + at // OUTER).astype(jnp.float32)
    other = lax.ppermute(
        jnp.where(odd, low, high), "ctx", [(i, i ^ 1) for i in range(count)]
    )
    key_rows = jnp.where(odd, other, low)
    value_rows = jnp.where(odd, high, other)
    ready = rotate_rows(key_rows.astype(jnp.float32), places).astype(jnp.bfloat16)
    part, lse = attend(asked, ready[None], value_rows[None])
    lse = lse[:, :, 0].reshape(count, rows // width, width)
    top = lax.reduce_precision(lse, 8, 7)
    rest = lse - top
    mid = lax.reduce_precision(rest, 8, 7)
    last = (rest - mid).astype(jnp.bfloat16)
    top, mid = top.astype(jnp.bfloat16), mid.astype(jnp.bfloat16)
    sent = lax.all_to_all(
        jnp.concatenate([part, top, mid, last], axis=1),
        "ctx",
        split_axis=0,
        concat_axis=0,
        tiled=True,
    )
    got = sent[:, :rows].astype(jnp.float32).reshape(heads, 2, rows, width)
    logs = jnp.sum(
        sent[:, rows:].astype(jnp.float32).reshape(heads, 2, 3, rows), axis=2
    )
    share = jax.nn.sigmoid((logs[:, 0] - logs[:, 1]) * math.log(2.0))[..., None]
    return (got[:, 0] * share + got[:, 1] * (1.0 - share)).astype(jnp.bfloat16)


def by_columns(keys, values, queries, positions):
    key_parts = lax.all_to_all(keys, "ctx", split_axis=1, concat_axis=0, tiled=True)
    value_parts = lax.all_to_all(values, "ctx", split_axis=1, concat_axis=0, tiled=True)
    heads, rows, width = queries.shape
    per_device = key_parts.shape[1]
    compact = compress(jnp.concatenate([key_parts, value_parts], axis=1))
    rotated = rotate_rows(queries.astype(jnp.float32), positions.astype(jnp.float32)).astype(
        jnp.bfloat16
    )
    whole = lax.all_gather(compact.T, "ctx", axis=0, tiled=True)
    tokens = whole.shape[1]
    shaped = whole.reshape(-1, 2, per_device, tokens)
    key_rows = shaped[:, 0].reshape(heads, width, tokens).swapaxes(1, 2)
    value_rows = shaped[:, 1].reshape(heads, width, tokens).swapaxes(1, 2)
    places = jnp.arange(tokens).astype(jnp.float32)
    ready = rotate_rows(key_rows.astype(jnp.float32), places).astype(jnp.bfloat16)
    return attend(rotated, ready, value_rows)[0]


def solution(mesh):
    count = mesh.shape["ctx"]

    def on_device(keys, values, queries, positions):
        heads, rows, width = queries.shape
        if count == 2 * heads and rows % width == 0:
            return by_pairs(keys, values, queries, positions, count)
        return by_columns(keys, values, queries, positions)

    return jax.shard_map(
        on_device,
        mesh=mesh,
        in_specs=(
            P(("user", "ctx"), "heads"),
            P(("user", "ctx"), "heads"),
            P("heads", ("user", "ctx"), None),
            P(("user", "ctx")),
        ),
        out_specs=P("heads", ("user", "ctx"), None),
        check_vma=False,
    )
```

```python
import functools
import math

import jax
import jax.numpy as jnp
import numpy as np
from jax import lax
from jax.experimental import pallas as pl
from jax.experimental.pallas import tpu as pltpu
from jax.sharding import PartitionSpec as P

OUTER = 128


def split_two(matrix):
    high = matrix.astype(jnp.bfloat16)
    low = (matrix - np.asarray(high).astype(np.float64)).astype(jnp.bfloat16)
    return high, low


@functools.lru_cache(maxsize=None)
def stages(length):
    outer = OUTER
    inner = length // outer
    step = inner // 2
    a = np.arange(outer)
    c = np.arange(outer)
    turn = 2 * outer
    angle = np.pi / outer * ((c[:, None] * a[None, :]) % turn)
    alternate = np.where(a % 2 == 0, 1.0, -1.0)
    first = np.stack([np.cos(angle), -np.sin(angle)], axis=1)
    first[0, 1] = alternate
    d = np.arange(length // 2 // turn)
    k = np.concatenate([c[:, None] + turn * d, (turn - c[:, None]) % turn + turn * d], axis=1)
    k[0, d.size :] = outer + turn * d
    sign = np.concatenate([np.ones(d.size), -np.ones(d.size)])
    b = np.arange(inner)
    q = np.arange(step)
    theta = np.pi / (2 * length) * ((k[:, :, None] * (2 * b + 1)) % (4 * length))
    phi = np.pi / length * ((k[:, None, :] * (2 * q + 1)[:, None]) % (2 * length))
    forward = np.stack([np.cos(theta), np.sin(theta) * sign[None, :, None]], axis=2)
    weight = np.where(k == 0, 1.0, 2.0) / length
    back = np.stack([np.cos(phi), np.sin(phi) * sign], axis=1) * weight[:, None, None, :]
    half = d.size
    forward[0, :half, 1] = 0.0
    forward[0, half:, 1] = np.cos(theta[0, half:])
    forward[0, half:, 0] = 0.0
    back[0, 1, :, :half] = 0.0
    back[0, 1, :, half:] = np.cos(phi[0, :, half:]) * weight[0, half:]
    back[0, 0, :, half:] = 0.0
    middle = back.reshape(outer, 2 * step, 2 * half) @ forward.reshape(outer, 2 * half, 2 * inner)
    last = first.transpose(2, 0, 1).reshape(outer, 2 * outer)
    return first.reshape(2 * outer, outer), middle, last


def compress(signal):
    length, columns = signal.shape
    outer, inner = OUTER, length // OUTER
    first, middle, last = stages(length)
    first_high, first_low = split_two(first)
    flat = signal.reshape(outer, inner * columns)
    one = jnp.dot(first_high, flat, preferred_element_type=jnp.float32) + jnp.dot(
        first_low, flat, preferred_element_type=jnp.float32
    )
    one = one.reshape(outer, 2 * inner, columns)
    two = jnp.einsum(
        "cob,cbl->col", jnp.asarray(middle.astype(np.float32)), one, precision=lax.Precision.HIGH
    )
    three = jnp.dot(
        jnp.asarray(last.astype(np.float32)),
        two.reshape(2 * outer, inner // 2 * columns),
        precision=lax.Precision.HIGH,
    )
    return three.reshape(length // 2, columns).astype(jnp.bfloat16)

GAP = 8


def strict_dot(left, right):
    rows, columns = left.shape[0] // 2, right.shape[1]
    high = right.astype(jnp.bfloat16)
    low = (right - high.astype(jnp.float32)).astype(jnp.bfloat16)
    both = jnp.dot(
        left, jnp.concatenate([high, low], axis=1), preferred_element_type=jnp.float32
    )
    return both[:rows, :columns] + (both[:rows, columns:] + both[rows:, :columns])


def compress_kernel(
    inner,
    odd_ref,
    x_ref,
    first_ref,
    middle_ref,
    last_ref,
    coarse_ref,
    fine_ref,
    keep_ref,
    send_ref,
    wide_ref,
    one_ref,
):
    outer = OUTER
    step = inner // 2
    columns = x_ref.shape[1]
    here = pl.program_id(0)
    steps = pl.num_programs(0)
    per_step = middle_ref.shape[0]
    x_pitch = inner + GAP
    one_pitch = 2 * outer + GAP
    two_pitch = step + GAP

    @pl.when(here == 0)
    def _():
        def widen(a, carry):
            source = pl.multiple_of(a * inner, inner)
            wide_ref[pl.ds(pl.multiple_of(a * x_pitch, GAP), inner), :] = x_ref[
                pl.ds(source, inner), :
            ].astype(jnp.float32)
            return carry

        lax.fori_loop(0, outer, widen, 0, unroll=4)

        def stage_one(pair, carry):
            x = jnp.concatenate(
                [
                    wide_ref[pl.ds(2 * pair + i, outer, stride=x_pitch), :].astype(jnp.bfloat16)
                    for i in range(2)
                ],
                axis=1,
            )
            z = jnp.dot(
                first_ref[...],
                jnp.concatenate([x, x], axis=0),
                preferred_element_type=jnp.float32,
            )
            for i in range(2):
                start = pl.multiple_of((2 * pair + i) * one_pitch, GAP)
                one_ref[pl.ds(start, 2 * outer), :] = z[:, i * columns : (i + 1) * columns]
            return carry

        lax.fori_loop(0, inner // 2, stage_one, 0, unroll=4)

    for i in range(per_step):
        c = here * per_step + i
        z = jnp.concatenate(
            [
                one_ref[pl.ds(2 * c, inner, stride=one_pitch), :],
                one_ref[pl.ds(2 * c + 1, inner, stride=one_pitch), :],
            ],
            axis=0,
        )
        v = strict_dot(middle_ref[i], z)
        for part in range(2):
            wide_ref[pl.ds(pl.multiple_of((2 * c + part) * two_pitch, GAP), step), :] = v[
                part * step : (part + 1) * step
            ]

    @pl.when(here == steps - 1)
    def _():
        def stage_three(out_ref, offset):
            def one(i, carry):
                q = offset + i
                v = wide_ref[pl.ds(q, 2 * outer, stride=two_pitch), :]
                y = strict_dot(last_ref[...], v).astype(jnp.bfloat16).astype(jnp.float32)
                front = lax.broadcasted_iota(jnp.int32, y.shape, 1) < columns // 2
                cos_p, sin_p = coarse_ref[0], coarse_ref[1]
                cos_q, sin_q = fine_ref[0, pl.ds(q, 1), :], fine_ref[1, pl.ds(q, 1), :]
                sine = sin_p * cos_q + cos_p * sin_q
                other = pltpu.roll(y, columns // 2, 1)
                turned = y * (cos_p * cos_q - sin_p * sin_q) + other * jnp.where(
                    front, -sine, sine
                )
                out_ref[pl.ds(pl.multiple_of(i * outer, outer), outer), :] = turned.astype(
                    out_ref.dtype
                )
                return carry

            lax.fori_loop(0, step // 2, one, 0, unroll=4)

        odd = odd_ref[0]
        stage_three(send_ref, (1 - odd) * (step // 2))
        stage_three(keep_ref, odd * (step // 2))


def turns(places, width):
    angles = places[:, None] * inverse_freq(width)[None, :]
    cosine, sine = jnp.cos(angles), jnp.sin(angles)
    return jnp.stack(
        [jnp.concatenate([cosine, cosine], axis=1), jnp.concatenate([sine, sine], axis=1)]
    )


def compress_rows(signal, odd):
    length, columns = signal.shape
    outer, inner = OUTER, length // OUTER
    step = inner // 2
    first, middle, last = stages(length)
    first_pair = np.concatenate(split_two(first), axis=1)
    middle_pair = np.concatenate(split_two(middle), axis=1)
    last_pair = np.concatenate(split_two(last), axis=0)
    turned = (1 - odd).astype(jnp.float32)
    coarse = turns(jnp.arange(outer).astype(jnp.float32) * step * turned, columns)
    fine = turns(jnp.arange(step).astype(jnp.float32) * turned, columns)
    per_step = 8
    rows_wide = max(outer * (inner + GAP), 2 * outer * (step + GAP))
    once = pl.BlockSpec(memory_space=pltpu.VMEM)
    half = jax.ShapeDtypeStruct((length // 4, columns), jnp.bfloat16)
    return pl.pallas_call(
        functools.partial(compress_kernel, inner),
        grid=(outer // per_step,),
        in_specs=[
            pl.BlockSpec(memory_space=pltpu.SMEM),
            once,
            once,
            pl.BlockSpec((per_step, 2 * inner, 2 * inner), lambda i: (i, 0, 0)),
            once,
            once,
            once,
        ],
        out_specs=[once, once],
        out_shape=[half, half],
        scratch_shapes=[
            pltpu.VMEM((rows_wide, columns), jnp.float32),
            pltpu.VMEM((inner * (2 * outer + GAP), columns), jnp.float32),
        ],
        cost_estimate=pl.CostEstimate(
            flops=64 * length * outer * columns, bytes_accessed=16 * length * columns, transcendentals=0
        ),
    )(odd.reshape(1), signal, first_pair, middle_pair, last_pair, coarse, fine)


def inverse_freq(width):
    return jnp.exp(jnp.arange(width // 2).astype(jnp.float32) * (-2.0 * math.log(500000.0) / width))


def rotate_rows(block, places):
    width = block.shape[-1]
    half = width // 2
    angles = places[:, None] * inverse_freq(width)[None, :]
    cosine = jnp.cos(angles)
    sine = jnp.sin(angles)
    first = block[..., :half]
    second = block[..., half:]
    return jnp.concatenate(
        [first * cosine - second * sine, second * cosine + first * sine], axis=-1
    )


def attend_kernel(chunk, scale, swap_ref, q_ref, k_ref, v_ref, out_ref, lse_ref):
    q = q_ref[0]
    swap = swap_ref[0] == 1
    rows, width = q.shape
    factor = scale * math.log2(math.e)
    best = jnp.full((rows, 1), -jnp.inf, jnp.float32)
    total = jnp.zeros((rows, 1), jnp.float32)
    accum = jnp.zeros((rows, width), jnp.float32)
    tokens = k_ref.shape[1]
    for start in range(0, tokens, chunk):
        one = k_ref[0, start : start + chunk, :]
        two = v_ref[0, start : start + chunk, :]
        k, v = jnp.where(swap, two, one), jnp.where(swap, one, two)
        scores = lax.dot_general(
            q, k, (((1,), (1,)), ((), ())), preferred_element_type=jnp.float32
        )
        fresh = jnp.maximum(best, jnp.max(scores, axis=1, keepdims=True))
        expo = jnp.exp2((scores - fresh) * factor)
        shrink = jnp.exp2((best - fresh) * factor)
        total = total * shrink + jnp.sum(expo, axis=1, keepdims=True)
        accum = accum * shrink + jnp.dot(
            expo.astype(jnp.bfloat16), v, preferred_element_type=jnp.float32
        )
        best = fresh
    out_ref[0] = (accum / total).astype(out_ref.dtype)
    lse_ref[0] = jnp.broadcast_to(best * factor + jnp.log2(total), (rows, 8))


def attend(queries, keys, values, swap):
    groups, rows, width = queries.shape
    heads, tokens, _ = keys.shape
    per_head = groups // heads
    block = math.gcd(rows, 256)
    chunk = math.gcd(tokens, 1024)
    scale = 1.0 / math.sqrt(width)
    return pl.pallas_call(
        functools.partial(attend_kernel, chunk, scale),
        grid=(groups, rows // block),
        in_specs=[
            pl.BlockSpec(memory_space=pltpu.SMEM),
            pl.BlockSpec((1, block, width), lambda g, i: (g, i, 0)),
            pl.BlockSpec((1, tokens, width), lambda g, i: (g // per_head, 0, 0)),
            pl.BlockSpec((1, tokens, width), lambda g, i: (g // per_head, 0, 0)),
        ],
        out_specs=[
            pl.BlockSpec((1, block, width), lambda g, i: (g, i, 0)),
            pl.BlockSpec((1, block, 8), lambda g, i: (g, i, 0)),
        ],
        out_shape=[
            jax.ShapeDtypeStruct((groups, rows, width), jnp.bfloat16),
            jax.ShapeDtypeStruct((groups, rows, 8), jnp.float32),
        ],
        cost_estimate=pl.CostEstimate(
            flops=4 * groups * rows * tokens * width,
            bytes_accessed=2 * groups * rows * width * 2,
            transcendentals=groups * rows * tokens,
        ),
    )(swap.reshape(1), queries, keys, values)


def by_pairs(keys, values, queries, positions, count):
    heads, rows, width = queries.shape
    me = lax.axis_index("ctx")
    odd = (me % 2).astype(jnp.int32)
    pieces = []
    for head in range(heads):
        pieces.append(keys[:, head * width : (head + 1) * width])
        pieces.append(values[:, head * width : (head + 1) * width])
    mine = lax.all_to_all(jnp.stack(pieces), "ctx", split_axis=0, concat_axis=0, tiled=True)
    rotated = rotate_rows(queries.astype(jnp.float32), positions.astype(jnp.float32)).astype(
        jnp.bfloat16
    )
    asked = lax.all_to_all(
        jnp.repeat(rotated, 2, axis=0), "ctx", split_axis=0, concat_axis=0, tiled=True
    )
    keep, send = compress_rows(mine.reshape(-1, width), odd)
    other = lax.ppermute(send, "ctx", [(i, i ^ 1) for i in range(count)])
    part, lse = attend(asked, keep[None], other[None], odd)
    lse = lse[:, :, 0].reshape(count, rows // width, width)
    top = lax.reduce_precision(lse, 8, 7)
    rest = lse - top
    mid = lax.reduce_precision(rest, 8, 7)
    last = (rest - mid).astype(jnp.bfloat16)
    top, mid = top.astype(jnp.bfloat16), mid.astype(jnp.bfloat16)
    sent = lax.all_to_all(
        jnp.concatenate([part, top, mid, last], axis=1),
        "ctx",
        split_axis=0,
        concat_axis=0,
        tiled=True,
    )
    got = sent[:, :rows].astype(jnp.float32).reshape(heads, 2, rows, width)
    logs = jnp.sum(
        sent[:, rows:].astype(jnp.float32).reshape(heads, 2, 3, rows), axis=2
    )
    share = jax.nn.sigmoid((logs[:, 0] - logs[:, 1]) * math.log(2.0))[..., None]
    return (got[:, 0] * share + got[:, 1] * (1.0 - share)).astype(jnp.bfloat16)


def by_columns(keys, values, queries, positions):
    key_parts = lax.all_to_all(keys, "ctx", split_axis=1, concat_axis=0, tiled=True)
    value_parts = lax.all_to_all(values, "ctx", split_axis=1, concat_axis=0, tiled=True)
    heads, rows, width = queries.shape
    per_device = key_parts.shape[1]
    compact = compress(jnp.concatenate([key_parts, value_parts], axis=1))
    rotated = rotate_rows(queries.astype(jnp.float32), positions.astype(jnp.float32)).astype(
        jnp.bfloat16
    )
    whole = lax.all_gather(compact.T, "ctx", axis=0, tiled=True)
    tokens = whole.shape[1]
    shaped = whole.reshape(-1, 2, per_device, tokens)
    key_rows = shaped[:, 0].reshape(heads, width, tokens).swapaxes(1, 2)
    value_rows = shaped[:, 1].reshape(heads, width, tokens).swapaxes(1, 2)
    places = jnp.arange(tokens).astype(jnp.float32)
    ready = rotate_rows(key_rows.astype(jnp.float32), places).astype(jnp.bfloat16)
    return attend(rotated, ready, value_rows, jnp.zeros((), jnp.int32))[0]


def solution(mesh):
    count = mesh.shape["ctx"]

    def on_device(keys, values, queries, positions):
        heads, rows, width = queries.shape
        if count == 2 * heads and rows % width == 0:
            return by_pairs(keys, values, queries, positions, count)
        return by_columns(keys, values, queries, positions)

    return jax.shard_map(
        on_device,
        mesh=mesh,
        in_specs=(
            P(("user", "ctx"), "heads"),
            P(("user", "ctx"), "heads"),
            P("heads", ("user", "ctx"), None),
            P(("user", "ctx")),
        ),
        out_specs=P("heads", ("user", "ctx"), None),
        check_vma=False,
    )
```

```python
import functools
import math

import jax
import jax.numpy as jnp
import numpy as np
from jax import lax
from jax.experimental import pallas as pl
from jax.experimental.pallas import tpu as pltpu
from jax.sharding import PartitionSpec as P

OUTER = 128


def split_two(matrix):
    high = matrix.astype(jnp.bfloat16)
    low = (matrix - np.asarray(high).astype(np.float64)).astype(jnp.bfloat16)
    return high, low


@functools.lru_cache(maxsize=None)
def stages(length):
    outer = OUTER
    inner = length // outer
    step = inner // 2
    a = np.arange(outer)
    c = np.arange(outer)
    turn = 2 * outer
    angle = np.pi / outer * ((c[:, None] * a[None, :]) % turn)
    alternate = np.where(a % 2 == 0, 1.0, -1.0)
    first = np.stack([np.cos(angle), -np.sin(angle)], axis=1)
    first[0, 1] = alternate
    d = np.arange(length // 2 // turn)
    k = np.concatenate([c[:, None] + turn * d, (turn - c[:, None]) % turn + turn * d], axis=1)
    k[0, d.size :] = outer + turn * d
    sign = np.concatenate([np.ones(d.size), -np.ones(d.size)])
    b = np.arange(inner)
    q = np.arange(step)
    theta = np.pi / (2 * length) * ((k[:, :, None] * (2 * b + 1)) % (4 * length))
    phi = np.pi / length * ((k[:, None, :] * (2 * q + 1)[:, None]) % (2 * length))
    forward = np.stack([np.cos(theta), np.sin(theta) * sign[None, :, None]], axis=2)
    weight = np.where(k == 0, 1.0, 2.0) / length
    back = np.stack([np.cos(phi), np.sin(phi) * sign], axis=1) * weight[:, None, None, :]
    half = d.size
    forward[0, :half, 1] = 0.0
    forward[0, half:, 1] = np.cos(theta[0, half:])
    forward[0, half:, 0] = 0.0
    back[0, 1, :, :half] = 0.0
    back[0, 1, :, half:] = np.cos(phi[0, :, half:]) * weight[0, half:]
    back[0, 0, :, half:] = 0.0
    middle = back.reshape(outer, 2 * step, 2 * half) @ forward.reshape(outer, 2 * half, 2 * inner)
    last = first.transpose(2, 0, 1).reshape(outer, 2 * outer)
    return first.reshape(2 * outer, outer), middle, last


def compress(signal):
    length, columns = signal.shape
    outer, inner = OUTER, length // OUTER
    first, middle, last = stages(length)
    first_high, first_low = split_two(first)
    flat = signal.reshape(outer, inner * columns)
    one = jnp.dot(first_high, flat, preferred_element_type=jnp.float32) + jnp.dot(
        first_low, flat, preferred_element_type=jnp.float32
    )
    one = one.reshape(outer, 2 * inner, columns)
    two = jnp.einsum(
        "cob,cbl->col", jnp.asarray(middle.astype(np.float32)), one, precision=lax.Precision.HIGH
    )
    three = jnp.dot(
        jnp.asarray(last.astype(np.float32)),
        two.reshape(2 * outer, inner // 2 * columns),
        precision=lax.Precision.HIGH,
    )
    return three.reshape(length // 2, columns).astype(jnp.bfloat16)

GAP = 8


def strict_dot(left, right):
    rows, columns = left.shape[0] // 2, right.shape[1]
    high = right.astype(jnp.bfloat16)
    low = (right - high.astype(jnp.float32)).astype(jnp.bfloat16)
    both = jnp.dot(
        left, jnp.concatenate([high, low], axis=1), preferred_element_type=jnp.float32
    )
    return both[:rows, :columns] + (both[:rows, columns:] + both[rows:, :columns])


def compress_kernel(
    inner,
    odd_ref,
    x_ref,
    first_ref,
    middle_ref,
    last_ref,
    coarse_ref,
    fine_ref,
    keep_ref,
    send_one_ref,
    send_two_ref,
    wide_ref,
    one_ref,
):
    outer = OUTER
    step = inner // 2
    columns = x_ref.shape[1]
    here = pl.program_id(0)
    steps = pl.num_programs(0)
    per_step = middle_ref.shape[0]
    x_pitch = inner + GAP
    one_pitch = 2 * outer + GAP
    two_pitch = step + GAP

    @pl.when(here == 0)
    def _():
        def widen(a, carry):
            source = pl.multiple_of(a * inner, inner)
            wide_ref[pl.ds(pl.multiple_of(a * x_pitch, GAP), inner), :] = x_ref[
                pl.ds(source, inner), :
            ].astype(jnp.float32)
            return carry

        lax.fori_loop(0, outer, widen, 0, unroll=4)

        def stage_one(pair, carry):
            x = jnp.concatenate(
                [
                    wide_ref[pl.ds(2 * pair + i, outer, stride=x_pitch), :].astype(jnp.bfloat16)
                    for i in range(2)
                ],
                axis=1,
            )
            z = jnp.dot(
                first_ref[...],
                jnp.concatenate([x, x], axis=0),
                preferred_element_type=jnp.float32,
            )
            for i in range(2):
                start = pl.multiple_of((2 * pair + i) * one_pitch, GAP)
                one_ref[pl.ds(start, 2 * outer), :] = z[:, i * columns : (i + 1) * columns]
            return carry

        lax.fori_loop(0, inner // 2, stage_one, 0, unroll=4)

    for i in range(per_step):
        c = here * per_step + i
        z = jnp.concatenate(
            [
                one_ref[pl.ds(2 * c, inner, stride=one_pitch), :],
                one_ref[pl.ds(2 * c + 1, inner, stride=one_pitch), :],
            ],
            axis=0,
        )
        v = strict_dot(middle_ref[i], z)
        for part in range(2):
            wide_ref[pl.ds(pl.multiple_of((2 * c + part) * two_pitch, GAP), step), :] = v[
                part * step : (part + 1) * step
            ]

    @pl.when(here == steps - 1)
    def _():
        def stage_three(out_ref, offset):
            def one(i, carry):
                q = offset + i
                v = wide_ref[pl.ds(q, 2 * outer, stride=two_pitch), :]
                y = strict_dot(last_ref[...], v).astype(jnp.bfloat16).astype(jnp.float32)
                front = lax.broadcasted_iota(jnp.int32, y.shape, 1) < columns // 2
                cos_p, sin_p = coarse_ref[0], coarse_ref[1]
                cos_q, sin_q = fine_ref[0, pl.ds(q, 1), :], fine_ref[1, pl.ds(q, 1), :]
                sine = sin_p * cos_q + cos_p * sin_q
                other = pltpu.roll(y, columns // 2, 1)
                turned = y * (cos_p * cos_q - sin_p * sin_q) + other * jnp.where(
                    front, -sine, sine
                )
                out_ref[pl.ds(pl.multiple_of(i * outer, outer), outer), :] = turned.astype(
                    out_ref.dtype
                )
                return carry

            lax.fori_loop(0, out_ref.shape[0] // outer, one, 0, unroll=4)

        odd = odd_ref[0]
        stage_three(send_one_ref, (1 - odd) * (step // 2))
        stage_three(send_two_ref, (1 - odd) * (step // 2) + step // 4)
        stage_three(keep_ref, odd * (step // 2))


def turns(places, width):
    angles = places[:, None] * inverse_freq(width)[None, :]
    cosine, sine = jnp.cos(angles), jnp.sin(angles)
    return jnp.stack(
        [jnp.concatenate([cosine, cosine], axis=1), jnp.concatenate([sine, sine], axis=1)]
    )


def compress_rows(signal, odd):
    length, columns = signal.shape
    outer, inner = OUTER, length // OUTER
    step = inner // 2
    first, middle, last = stages(length)
    first_pair = np.concatenate(split_two(first), axis=1)
    middle_pair = np.concatenate(split_two(middle), axis=1)
    last_pair = np.concatenate(split_two(last), axis=0)
    turned = (1 - odd).astype(jnp.float32)
    coarse = turns(jnp.arange(outer).astype(jnp.float32) * step * turned, columns)
    fine = turns(jnp.arange(step).astype(jnp.float32) * turned, columns)
    per_step = 8
    rows_wide = max(outer * (inner + GAP), 2 * outer * (step + GAP))
    once = pl.BlockSpec(memory_space=pltpu.VMEM)
    half = jax.ShapeDtypeStruct((length // 4, columns), jnp.bfloat16)
    quarter = jax.ShapeDtypeStruct((length // 8, columns), jnp.bfloat16)
    return pl.pallas_call(
        functools.partial(compress_kernel, inner),
        grid=(outer // per_step,),
        in_specs=[
            pl.BlockSpec(memory_space=pltpu.SMEM),
            once,
            once,
            pl.BlockSpec((per_step, 2 * inner, 2 * inner), lambda i: (i, 0, 0)),
            once,
            once,
            once,
        ],
        out_specs=[once, once, once],
        out_shape=[half, quarter, quarter],
        scratch_shapes=[
            pltpu.VMEM((rows_wide, columns), jnp.float32),
            pltpu.VMEM((inner * (2 * outer + GAP), columns), jnp.float32),
        ],
        cost_estimate=pl.CostEstimate(
            flops=64 * length * outer * columns, bytes_accessed=16 * length * columns, transcendentals=0
        ),
    )(odd.reshape(1), signal, first_pair, middle_pair, last_pair, coarse, fine)


def inverse_freq(width):
    return jnp.exp(jnp.arange(width // 2).astype(jnp.float32) * (-2.0 * math.log(500000.0) / width))


def rotate_rows(block, places):
    width = block.shape[-1]
    half = width // 2
    angles = places[:, None] * inverse_freq(width)[None, :]
    cosine = jnp.cos(angles)
    sine = jnp.sin(angles)
    first = block[..., :half]
    second = block[..., half:]
    return jnp.concatenate(
        [first * cosine - second * sine, second * cosine + first * sine], axis=-1
    )


def attend_kernel(chunk, scale, resume, finish, swap_ref, q_ref, k_ref, v_ref, *refs):
    q = q_ref[0]
    swap = swap_ref[0] == 1
    rows, width = q.shape
    factor = scale * math.log2(math.e)
    if resume:
        accum = refs[0][0]
        best = refs[1][0][:, :1]
        total = refs[2][0][:, :1]
        refs = refs[3:]
    else:
        best = jnp.full((rows, 1), -jnp.inf, jnp.float32)
        total = jnp.zeros((rows, 1), jnp.float32)
        accum = jnp.zeros((rows, width), jnp.float32)
    tokens = k_ref.shape[1]
    for start in range(0, tokens, chunk):
        one = k_ref[0, start : start + chunk, :]
        two = v_ref[0, start : start + chunk, :]
        k, v = jnp.where(swap, two, one), jnp.where(swap, one, two)
        scores = lax.dot_general(
            q, k, (((1,), (1,)), ((), ())), preferred_element_type=jnp.float32
        )
        fresh = jnp.maximum(best, jnp.max(scores, axis=1, keepdims=True))
        expo = jnp.exp2((scores - fresh) * factor)
        shrink = jnp.exp2((best - fresh) * factor)
        total = total * shrink + jnp.sum(expo, axis=1, keepdims=True)
        accum = accum * shrink + jnp.dot(
            expo.astype(jnp.bfloat16), v, preferred_element_type=jnp.float32
        )
        best = fresh
    if finish:
        refs[0][0] = (accum / total).astype(refs[0].dtype)
        refs[1][0] = jnp.broadcast_to(best * factor + jnp.log2(total), (rows, 8))
    else:
        refs[0][0] = accum
        refs[1][0] = jnp.broadcast_to(best, (rows, 8))
        refs[2][0] = jnp.broadcast_to(total, (rows, 8))


def attend(queries, keys, values, swap, part=0, parts=1, state=None):
    groups, rows, width = queries.shape
    heads, tokens, _ = values.shape
    per_head = groups // heads
    block = math.gcd(rows, 256)
    chunk = math.gcd(tokens, 1024)
    scale = 1.0 / math.sqrt(width)
    finish = part == parts - 1
    wide = pl.BlockSpec((1, block, width), lambda g, i: (g, i, 0))
    thin = pl.BlockSpec((1, block, 8), lambda g, i: (g, i, 0))
    thin_shape = jax.ShapeDtypeStruct((groups, rows, 8), jnp.float32)
    state = () if state is None else tuple(state)
    wide_type = jnp.bfloat16 if finish else jnp.float32
    return pl.pallas_call(
        functools.partial(attend_kernel, chunk, scale, bool(state), finish),
        grid=(groups, rows // block),
        in_specs=[
            pl.BlockSpec(memory_space=pltpu.SMEM),
            wide,
            pl.BlockSpec((1, tokens, width), lambda g, i: (g // per_head, part, 0)),
            pl.BlockSpec((1, tokens, width), lambda g, i: (g // per_head, 0, 0)),
        ]
        + ([wide, thin, thin] if state else []),
        out_specs=[wide, thin] if finish else [wide, thin, thin],
        out_shape=[jax.ShapeDtypeStruct((groups, rows, width), wide_type), thin_shape]
        + ([] if finish else [thin_shape]),
        cost_estimate=pl.CostEstimate(
            flops=8 * groups * rows * tokens * width,
            bytes_accessed=4 * groups * rows * width * 2,
            transcendentals=groups * rows * tokens,
        ),
    )(swap.reshape(1), queries, keys, values, *state)


def stack_kernel(keys_ref, values_ref, out_ref):
    width = out_ref.shape[2]
    for head in range(out_ref.shape[0] // 2):
        columns = slice(head * width, (head + 1) * width)
        out_ref[2 * head] = keys_ref[:, columns]
        out_ref[2 * head + 1] = values_ref[:, columns]


def stack(keys, values, width):
    rows, columns = keys.shape
    pieces = 2 * columns // width
    block = math.gcd(rows, 512)
    spec = pl.BlockSpec((block, columns), lambda i: (i, 0))
    return pl.pallas_call(
        stack_kernel,
        grid=(rows // block,),
        in_specs=[spec, spec],
        out_specs=pl.BlockSpec((pieces, block, width), lambda i: (0, i, 0)),
        out_shape=jax.ShapeDtypeStruct((pieces, rows, width), keys.dtype),
    )(keys, values)


def by_pairs(keys, values, queries, positions, count):
    heads, rows, width = queries.shape
    me = lax.axis_index("ctx")
    odd = (me % 2).astype(jnp.int32)
    mine = lax.all_to_all(
        stack(keys, values, width), "ctx", split_axis=0, concat_axis=0, tiled=True
    )
    rotated = rotate_rows(queries.astype(jnp.float32), positions.astype(jnp.float32)).astype(
        jnp.bfloat16
    )
    asked = lax.all_to_all(
        jnp.repeat(rotated, 2, axis=0), "ctx", split_axis=0, concat_axis=0, tiled=True
    )
    keep, *sends = compress_rows(mine.reshape(-1, width), odd)
    pairs = [(i, i ^ 1) for i in range(count)]
    others = [lax.ppermute(send, "ctx", pairs) for send in sends]
    state = None
    for part, other in enumerate(others):
        state = attend(asked, keep[None], other[None], odd, part, len(others), state)
    part, lse = state
    lse = lse[:, :, 0].reshape(count, rows // width, width)
    top = lax.reduce_precision(lse, 8, 7)
    rest = lse - top
    mid = lax.reduce_precision(rest, 8, 7)
    last = (rest - mid).astype(jnp.bfloat16)
    top, mid = top.astype(jnp.bfloat16), mid.astype(jnp.bfloat16)
    sent = lax.all_to_all(
        jnp.concatenate([part, top, mid, last], axis=1),
        "ctx",
        split_axis=0,
        concat_axis=0,
        tiled=True,
    )
    got = sent[:, :rows].astype(jnp.float32).reshape(heads, 2, rows, width)
    logs = jnp.sum(
        sent[:, rows:].astype(jnp.float32).reshape(heads, 2, 3, rows), axis=2
    )
    share = jax.nn.sigmoid((logs[:, 0] - logs[:, 1]) * math.log(2.0))[..., None]
    return (got[:, 0] * share + got[:, 1] * (1.0 - share)).astype(jnp.bfloat16)


def by_columns(keys, values, queries, positions):
    key_parts = lax.all_to_all(keys, "ctx", split_axis=1, concat_axis=0, tiled=True)
    value_parts = lax.all_to_all(values, "ctx", split_axis=1, concat_axis=0, tiled=True)
    heads, rows, width = queries.shape
    per_device = key_parts.shape[1]
    compact = compress(jnp.concatenate([key_parts, value_parts], axis=1))
    rotated = rotate_rows(queries.astype(jnp.float32), positions.astype(jnp.float32)).astype(
        jnp.bfloat16
    )
    whole = lax.all_gather(compact.T, "ctx", axis=0, tiled=True)
    tokens = whole.shape[1]
    shaped = whole.reshape(-1, 2, per_device, tokens)
    key_rows = shaped[:, 0].reshape(heads, width, tokens).swapaxes(1, 2)
    value_rows = shaped[:, 1].reshape(heads, width, tokens).swapaxes(1, 2)
    places = jnp.arange(tokens).astype(jnp.float32)
    ready = rotate_rows(key_rows.astype(jnp.float32), places).astype(jnp.bfloat16)
    return attend(rotated, ready, value_rows, jnp.zeros((), jnp.int32))[0]


def solution(mesh):
    count = mesh.shape["ctx"]

    def on_device(keys, values, queries, positions):
        heads, rows, width = queries.shape
        if count == 2 * heads and rows % width == 0:
            return by_pairs(keys, values, queries, positions, count)
        return by_columns(keys, values, queries, positions)

    return jax.shard_map(
        on_device,
        mesh=mesh,
        in_specs=(
            P(("user", "ctx"), "heads"),
            P(("user", "ctx"), "heads"),
            P("heads", ("user", "ctx"), None),
            P(("user", "ctx")),
        ),
        out_specs=P("heads", ("user", "ctx"), None),
        check_vma=False,
    )
```

```python
import functools
import math

import jax
import jax.numpy as jnp
import numpy as np
from jax import lax
from jax.experimental import pallas as pl
from jax.experimental.pallas import tpu as pltpu
from jax.sharding import PartitionSpec as P

OUTER = 128


def split_two(matrix):
    high = matrix.astype(jnp.bfloat16)
    low = (matrix - np.asarray(high).astype(np.float64)).astype(jnp.bfloat16)
    return high, low


@functools.lru_cache(maxsize=None)
def stages(length):
    outer = OUTER
    inner = length // outer
    step = inner // 2
    a = np.arange(outer)
    c = np.arange(outer)
    turn = 2 * outer
    angle = np.pi / outer * ((c[:, None] * a[None, :]) % turn)
    alternate = np.where(a % 2 == 0, 1.0, -1.0)
    first = np.stack([np.cos(angle), -np.sin(angle)], axis=1)
    first[0, 1] = alternate
    d = np.arange(length // 2 // turn)
    k = np.concatenate([c[:, None] + turn * d, (turn - c[:, None]) % turn + turn * d], axis=1)
    k[0, d.size :] = outer + turn * d
    sign = np.concatenate([np.ones(d.size), -np.ones(d.size)])
    b = np.arange(inner)
    q = np.arange(step)
    theta = np.pi / (2 * length) * ((k[:, :, None] * (2 * b + 1)) % (4 * length))
    phi = np.pi / length * ((k[:, None, :] * (2 * q + 1)[:, None]) % (2 * length))
    forward = np.stack([np.cos(theta), np.sin(theta) * sign[None, :, None]], axis=2)
    weight = np.where(k == 0, 1.0, 2.0) / length
    back = np.stack([np.cos(phi), np.sin(phi) * sign], axis=1) * weight[:, None, None, :]
    half = d.size
    forward[0, :half, 1] = 0.0
    forward[0, half:, 1] = np.cos(theta[0, half:])
    forward[0, half:, 0] = 0.0
    back[0, 1, :, :half] = 0.0
    back[0, 1, :, half:] = np.cos(phi[0, :, half:]) * weight[0, half:]
    back[0, 0, :, half:] = 0.0
    middle = back.reshape(outer, 2 * step, 2 * half) @ forward.reshape(outer, 2 * half, 2 * inner)
    last = first.transpose(2, 0, 1).reshape(outer, 2 * outer)
    return first.reshape(2 * outer, outer), middle, last


def compress(signal):
    length, columns = signal.shape
    outer, inner = OUTER, length // OUTER
    first, middle, last = stages(length)
    first_high, first_low = split_two(first)
    flat = signal.reshape(outer, inner * columns)
    one = jnp.dot(first_high, flat, preferred_element_type=jnp.float32) + jnp.dot(
        first_low, flat, preferred_element_type=jnp.float32
    )
    one = one.reshape(outer, 2 * inner, columns)
    two = jnp.einsum(
        "cob,cbl->col", jnp.asarray(middle.astype(np.float32)), one, precision=lax.Precision.HIGH
    )
    three = jnp.dot(
        jnp.asarray(last.astype(np.float32)),
        two.reshape(2 * outer, inner // 2 * columns),
        precision=lax.Precision.HIGH,
    )
    return three.reshape(length // 2, columns).astype(jnp.bfloat16)

GAP = 8


def strict_dot(left, right):
    rows, columns = left.shape[0] // 2, right.shape[1]
    high = right.astype(jnp.bfloat16)
    low = (right - high.astype(jnp.float32)).astype(jnp.bfloat16)
    both = jnp.dot(
        left, jnp.concatenate([high, low], axis=1), preferred_element_type=jnp.float32
    )
    return both[:rows, :columns] + (both[:rows, columns:] + both[rows:, :columns])


def compress_kernel(
    inner,
    odd_ref,
    x_ref,
    first_ref,
    middle_ref,
    last_ref,
    coarse_ref,
    fine_ref,
    keep_ref,
    send_one_ref,
    send_two_ref,
    wide_ref,
    one_ref,
):
    outer = OUTER
    step = inner // 2
    columns = x_ref.shape[1]
    here = pl.program_id(0)
    steps = pl.num_programs(0)
    per_step = middle_ref.shape[0]
    x_pitch = inner + GAP
    one_pitch = 2 * outer + GAP
    two_pitch = step + GAP

    @pl.when(here == 0)
    def _():
        def widen(a, carry):
            source = pl.multiple_of(a * inner, inner)
            wide_ref[pl.ds(pl.multiple_of(a * x_pitch, GAP), inner), :] = x_ref[
                pl.ds(source, inner), :
            ].astype(jnp.float32)
            return carry

        lax.fori_loop(0, outer, widen, 0, unroll=4)

        def stage_one(pair, carry):
            x = jnp.concatenate(
                [
                    wide_ref[pl.ds(2 * pair + i, outer, stride=x_pitch), :].astype(jnp.bfloat16)
                    for i in range(2)
                ],
                axis=1,
            )
            z = jnp.dot(
                first_ref[...],
                jnp.concatenate([x, x], axis=0),
                preferred_element_type=jnp.float32,
            )
            for i in range(2):
                start = pl.multiple_of((2 * pair + i) * one_pitch, GAP)
                one_ref[pl.ds(start, 2 * outer), :] = z[:, i * columns : (i + 1) * columns]
            return carry

        lax.fori_loop(0, inner // 2, stage_one, 0, unroll=4)

    for i in range(per_step):
        c = here * per_step + i
        z = jnp.concatenate(
            [
                one_ref[pl.ds(2 * c, inner, stride=one_pitch), :],
                one_ref[pl.ds(2 * c + 1, inner, stride=one_pitch), :],
            ],
            axis=0,
        )
        v = strict_dot(middle_ref[i], z)
        for part in range(2):
            wide_ref[pl.ds(pl.multiple_of((2 * c + part) * two_pitch, GAP), step), :] = v[
                part * step : (part + 1) * step
            ]

    @pl.when(here == steps - 1)
    def _():
        def stage_three(out_ref, offset):
            def one(i, carry):
                q = offset + i
                v = wide_ref[pl.ds(q, 2 * outer, stride=two_pitch), :]
                y = strict_dot(last_ref[...], v).astype(jnp.bfloat16).astype(jnp.float32)
                front = lax.broadcasted_iota(jnp.int32, y.shape, 1) < columns // 2
                cos_p, sin_p = coarse_ref[0], coarse_ref[1]
                cos_q, sin_q = fine_ref[0, pl.ds(q, 1), :], fine_ref[1, pl.ds(q, 1), :]
                sine = sin_p * cos_q + cos_p * sin_q
                other = pltpu.roll(y, columns // 2, 1)
                turned = y * (cos_p * cos_q - sin_p * sin_q) + other * jnp.where(
                    front, -sine, sine
                )
                out_ref[pl.ds(pl.multiple_of(i * outer, outer), outer), :] = turned.astype(
                    out_ref.dtype
                )
                return carry

            lax.fori_loop(0, out_ref.shape[0] // outer, one, 0, unroll=4)

        odd = odd_ref[0]
        stage_three(send_one_ref, (1 - odd) * (step // 2))
        stage_three(send_two_ref, (1 - odd) * (step // 2) + step // 4)
        stage_three(keep_ref, odd * (step // 2))


def turns(places, width):
    angles = places[:, None] * inverse_freq(width)[None, :]
    cosine, sine = jnp.cos(angles), jnp.sin(angles)
    return jnp.stack(
        [jnp.concatenate([cosine, cosine], axis=1), jnp.concatenate([sine, sine], axis=1)]
    )


def compress_rows(signal, odd):
    length, columns = signal.shape
    outer, inner = OUTER, length // OUTER
    step = inner // 2
    first, middle, last = stages(length)
    first_pair = np.concatenate(split_two(first), axis=1)
    middle_pair = np.concatenate(split_two(middle), axis=1)
    last_pair = np.concatenate(split_two(last), axis=0)
    turned = (1 - odd).astype(jnp.float32)
    coarse = turns(jnp.arange(outer).astype(jnp.float32) * step * turned, columns)
    fine = turns(jnp.arange(step).astype(jnp.float32) * turned, columns)
    per_step = 8
    rows_wide = max(outer * (inner + GAP), 2 * outer * (step + GAP))
    once = pl.BlockSpec(memory_space=pltpu.VMEM)
    half = jax.ShapeDtypeStruct((length // 4, columns), jnp.bfloat16)
    quarter = jax.ShapeDtypeStruct((length // 8, columns), jnp.bfloat16)
    return pl.pallas_call(
        functools.partial(compress_kernel, inner),
        grid=(outer // per_step,),
        in_specs=[
            pl.BlockSpec(memory_space=pltpu.SMEM),
            once,
            once,
            pl.BlockSpec((per_step, 2 * inner, 2 * inner), lambda i: (i, 0, 0)),
            once,
            once,
            once,
        ],
        out_specs=[once, once, once],
        out_shape=[half, quarter, quarter],
        scratch_shapes=[
            pltpu.VMEM((rows_wide, columns), jnp.float32),
            pltpu.VMEM((inner * (2 * outer + GAP), columns), jnp.float32),
        ],
        cost_estimate=pl.CostEstimate(
            flops=64 * length * outer * columns, bytes_accessed=16 * length * columns, transcendentals=0
        ),
    )(odd.reshape(1), signal, first_pair, middle_pair, last_pair, coarse, fine)


def inverse_freq(width):
    return jnp.exp(jnp.arange(width // 2).astype(jnp.float32) * (-2.0 * math.log(500000.0) / width))


def rotate_rows(block, places):
    width = block.shape[-1]
    half = width // 2
    angles = places[:, None] * inverse_freq(width)[None, :]
    cosine = jnp.cos(angles)
    sine = jnp.sin(angles)
    first = block[..., :half]
    second = block[..., half:]
    return jnp.concatenate(
        [first * cosine - second * sine, second * cosine + first * sine], axis=-1
    )


def attend_kernel(chunk, scale, resume, finish, swap_ref, q_ref, k_ref, v_ref, *refs):
    q = q_ref[0]
    swap = swap_ref[0] == 1
    rows, width = q.shape
    factor = scale * math.log2(math.e)
    if resume:
        accum = refs[0][0]
        best = refs[1][0][:, :1]
        total = refs[2][0][:, :1]
        refs = refs[3:]
    else:
        best = jnp.full((rows, 1), -jnp.inf, jnp.float32)
        total = jnp.zeros((rows, 1), jnp.float32)
        accum = jnp.zeros((rows, width), jnp.float32)
    tokens = k_ref.shape[1]
    for start in range(0, tokens, chunk):
        one = k_ref[0, start : start + chunk, :]
        two = v_ref[0, start : start + chunk, :]
        k, v = jnp.where(swap, two, one), jnp.where(swap, one, two)
        scores = lax.dot_general(
            q, k, (((1,), (1,)), ((), ())), preferred_element_type=jnp.float32
        )
        fresh = jnp.maximum(best, jnp.max(scores, axis=1, keepdims=True))
        expo = jnp.exp2((scores - fresh) * factor)
        shrink = jnp.exp2((best - fresh) * factor)
        total = total * shrink + jnp.sum(expo, axis=1, keepdims=True)
        accum = accum * shrink + jnp.dot(
            expo.astype(jnp.bfloat16), v, preferred_element_type=jnp.float32
        )
        best = fresh
    if finish:
        refs[0][0] = (accum / total).astype(refs[0].dtype)
        refs[1][0] = jnp.broadcast_to(best * factor + jnp.log2(total), (rows, 8))
    else:
        refs[0][0] = accum
        refs[1][0] = jnp.broadcast_to(best, (rows, 8))
        refs[2][0] = jnp.broadcast_to(total, (rows, 8))


def attend(queries, keys, values, swap, part=0, parts=1, state=None):
    groups, rows, width = queries.shape
    heads, tokens, _ = values.shape
    per_head = groups // heads
    block = math.gcd(rows, 768)
    chunk = math.gcd(tokens, 1024)
    scale = 1.0 / math.sqrt(width)
    finish = part == parts - 1
    wide = pl.BlockSpec((1, block, width), lambda g, i: (g, i, 0))
    thin = pl.BlockSpec((1, block, 8), lambda g, i: (g, i, 0))
    thin_shape = jax.ShapeDtypeStruct((groups, rows, 8), jnp.float32)
    state = () if state is None else tuple(state)
    wide_type = jnp.bfloat16 if finish else jnp.float32
    return pl.pallas_call(
        functools.partial(attend_kernel, chunk, scale, bool(state), finish),
        grid=(groups, rows // block),
        in_specs=[
            pl.BlockSpec(memory_space=pltpu.SMEM),
            wide,
            pl.BlockSpec((1, tokens, width), lambda g, i: (g // per_head, part, 0)),
            pl.BlockSpec((1, tokens, width), lambda g, i: (g // per_head, 0, 0)),
        ]
        + ([wide, thin, thin] if state else []),
        out_specs=[wide, thin] if finish else [wide, thin, thin],
        out_shape=[jax.ShapeDtypeStruct((groups, rows, width), wide_type), thin_shape]
        + ([] if finish else [thin_shape]),
        cost_estimate=pl.CostEstimate(
            flops=8 * groups * rows * tokens * width,
            bytes_accessed=4 * groups * rows * width * 2,
            transcendentals=groups * rows * tokens,
        ),
    )(swap.reshape(1), queries, keys, values, *state)


def by_pairs(keys, values, queries, positions, count):
    heads, rows, width = queries.shape
    me = lax.axis_index("ctx")
    odd = (me % 2).astype(jnp.int32)
    pieces = []
    for head in range(heads):
        pieces.append(keys[:, head * width : (head + 1) * width])
        pieces.append(values[:, head * width : (head + 1) * width])
    mine = lax.all_to_all(jnp.stack(pieces), "ctx", split_axis=0, concat_axis=0, tiled=True)
    rotated = rotate_rows(queries.astype(jnp.float32), positions.astype(jnp.float32)).astype(
        jnp.bfloat16
    )
    asked = lax.all_to_all(
        jnp.repeat(rotated, 2, axis=0), "ctx", split_axis=0, concat_axis=0, tiled=True
    )
    keep, *sends = compress_rows(mine.reshape(-1, width), odd)
    pairs = [(i, i ^ 1) for i in range(count)]
    others = [lax.ppermute(send, "ctx", pairs) for send in sends]
    state = None
    for part, other in enumerate(others):
        state = attend(asked, keep[None], other[None], odd, part, len(others), state)
    part, lse = state
    lse = lse[:, :, 0].reshape(count, rows // width, width)
    top = lax.reduce_precision(lse, 8, 7)
    rest = lse - top
    mid = lax.reduce_precision(rest, 8, 7)
    last = (rest - mid).astype(jnp.bfloat16)
    top, mid = top.astype(jnp.bfloat16), mid.astype(jnp.bfloat16)
    sent = lax.all_to_all(
        jnp.concatenate([part, top, mid, last], axis=1),
        "ctx",
        split_axis=0,
        concat_axis=0,
        tiled=True,
    )
    got = sent[:, :rows].astype(jnp.float32).reshape(heads, 2, rows, width)
    logs = jnp.sum(
        sent[:, rows:].astype(jnp.float32).reshape(heads, 2, 3, rows), axis=2
    )
    share = jax.nn.sigmoid((logs[:, 0] - logs[:, 1]) * math.log(2.0))[..., None]
    return (got[:, 0] * share + got[:, 1] * (1.0 - share)).astype(jnp.bfloat16)


def by_columns(keys, values, queries, positions):
    key_parts = lax.all_to_all(keys, "ctx", split_axis=1, concat_axis=0, tiled=True)
    value_parts = lax.all_to_all(values, "ctx", split_axis=1, concat_axis=0, tiled=True)
    heads, rows, width = queries.shape
    per_device = key_parts.shape[1]
    compact = compress(jnp.concatenate([key_parts, value_parts], axis=1))
    rotated = rotate_rows(queries.astype(jnp.float32), positions.astype(jnp.float32)).astype(
        jnp.bfloat16
    )
    whole = lax.all_gather(compact.T, "ctx", axis=0, tiled=True)
    tokens = whole.shape[1]
    shaped = whole.reshape(-1, 2, per_device, tokens)
    key_rows = shaped[:, 0].reshape(heads, width, tokens).swapaxes(1, 2)
    value_rows = shaped[:, 1].reshape(heads, width, tokens).swapaxes(1, 2)
    places = jnp.arange(tokens).astype(jnp.float32)
    ready = rotate_rows(key_rows.astype(jnp.float32), places).astype(jnp.bfloat16)
    return attend(rotated, ready, value_rows, jnp.zeros((), jnp.int32))[0]


def solution(mesh):
    count = mesh.shape["ctx"]

    def on_device(keys, values, queries, positions):
        heads, rows, width = queries.shape
        if count == 2 * heads and rows % width == 0:
            return by_pairs(keys, values, queries, positions, count)
        return by_columns(keys, values, queries, positions)

    return jax.shard_map(
        on_device,
        mesh=mesh,
        in_specs=(
            P(("user", "ctx"), "heads"),
            P(("user", "ctx"), "heads"),
            P("heads", ("user", "ctx"), None),
            P(("user", "ctx")),
        ),
        out_specs=P("heads", ("user", "ctx"), None),
        check_vma=False,
    )
```
